32 devices in a mesh: section: 8 (over z, x), replica: 4 (over y, core).
Axes of the slice: x: 2, y: 2, z: 4, core: 2. Of those that a mesh axis runs over, the one named last changes fastest.
Arguments:
- wa_local: bfloat16 [8, 4, 576, 1536], P('section', 'replica'), may hold values from -0.25 to 0.25
- wb_local: bfloat16 [8, 4, 1536, 576], P('section', 'replica'), may hold values from -0.15625 to 0.15625
- wa_master: float32 [8, 576, 1536], P('section', 'replica'), may hold values from -0.25 to 0.25
- wb_master: float32 [8, 1536, 576], P('section', None, 'replica'), may hold values from -0.15625 to 0.15625
- wa_moment: float32 [8, 576, 1536], P('section', 'replica'), may hold values from -0.075 to 0.075
- wb_moment: float32 [8, 1536, 576], P('section', None, 'replica'), may hold values from -0.045927934 to 0.045927934
- counts: int32 [8], P('section'), may hold values from 1 to 6
- inputs: bfloat16 [1024, 576], P('replica'), may hold values from -6 to 6
Outputs:
- wa_next: float32 [8, 576, 1536], P('section', 'replica')
- wb_next: float32 [8, 1536, 576], P('section', None, 'replica')
- boundary: bfloat16 [8, 1024, 576], P('section', 'replica')
The draws below stay inside these ranges and needn't reach their ends.
Inputs may be any that keep to these rules, and one draw needn't show every extreme that they name: `counts`: each section applies its layer at least once and at most 6 times.
All inputs are finite; a program needn't handle non-finite values.
Results may differ from the reference program's by a relative error of at most 0.03.
Values may be sent and summed in bfloat16 or wider, within the bound.
A program may use at most 64 MiB of HBM per device.

```python
import jax
import jax.numpy as jnp
from jax import lax

D = 576
FS = 1536
MOST_LAYERS = 6
TOKENS = 1024
N_SECTION = 8
N_REPLICA = 4


def touch_ends(entries, key, smallest, largest):
    longest = entries.shape.index(max(entries.shape))
    spots = []
    for shift in (0, 1):
        where = [jax.random.randint(jax.random.fold_in(key, axis), (), 0, length) for axis, length in enumerate(entries.shape)]
        where[longest] = (where[longest] + shift) % entries.shape[longest]
        spots.append(tuple(where))
    return entries.at[spots[0]].set(smallest).at[spots[1]].set(largest)


def block_scale(key, dims, cuts, low, largest):
    loudness, own = 1.0, jax.random.fold_in(key, 6)
    for axis_at, blocks in cuts:
        draws = jnp.exp(jax.random.uniform(jax.random.fold_in(own, axis_at), (blocks,), jnp.float32, low / len(cuts), largest / len(cuts)))
        loudness = loudness * jnp.repeat(draws, dims[axis_at] // blocks).reshape([-1 if axis == axis_at else 1 for axis in range(len(dims))])
    return loudness


def gaussian(stream_key, shape, scale, most, shards=(), kind=jnp.bfloat16):
    entries = scale * jax.random.normal(stream_key, shape, jnp.float32)
    if shards:
        entries = entries * block_scale(stream_key, shape, shards, -0.22, 0.18)
    return jnp.clip(entries, -most, most).astype(kind)


def setup_inputs(seed: int = 0) -> dict:
    key_of = jax.random.split(jax.random.key(seed), 9)
    wa_local = gaussian(key_of[0], (N_SECTION, N_REPLICA, D, FS), D ** -0.5, 0.25, ((0, 8), (1, 4)))
    wb_local = gaussian(key_of[1], (N_SECTION, N_REPLICA, FS, D), FS ** -0.5, 0.15625, ((0, 8), (1, 4)))
    wa_master = gaussian(key_of[2], (N_SECTION, D, FS), D ** -0.5, 0.25, ((0, 8), (1, 4)), jnp.float32)
    wb_master = gaussian(key_of[3], (N_SECTION, FS, D), FS ** -0.5, 0.15625, ((0, 8), (2, 4)), jnp.float32)
    wa_moment = gaussian(key_of[4], (N_SECTION, D, FS), (0.3 * D ** -0.5), 0.075, ((0, 8), (1, 4)), jnp.float32)
    wb_moment = gaussian(key_of[5], (N_SECTION, FS, D), (0.3 * FS ** -0.5), 0.045927934, ((0, 8), (2, 4)), jnp.float32)
    counts = touch_ends(jax.random.randint(key_of[6], (N_SECTION,), 1, MOST_LAYERS + 1), jax.random.fold_in(key_of[6], 1), 1, MOST_LAYERS).astype(jnp.int32)
    inputs = gaussian(key_of[7], (TOKENS, D), 1.0, 6.0, ((0, 4),))
    return dict(wa_local=wa_local, wb_local=wb_local, wa_master=wa_master, wb_master=wb_master, wa_moment=wa_moment, wb_moment=wb_moment, counts=counts, inputs=inputs)


def outer_update(master, moment, local):
    summed = lax.optimization_barrier(jnp.sum(local.astype(jnp.float32), axis=0))
    mean_value = summed / N_REPLICA
    delta = master - mean_value
    moment_new = 0.9 * moment + delta
    return master - 0.7 * (delta + 0.9 * moment_new)

def run_section(rows_in, layer_count, wa_bf, wb_bf):

    def apply_layer(step_index, stream):
        square_mean = lax.optimization_barrier(jnp.mean(stream * stream, axis=-1, keepdims=True))
        normed = (stream * lax.rsqrt(square_mean + 1e-05)).astype(jnp.bfloat16)
        gate_value = jnp.dot(normed, wa_bf, preferred_element_type=jnp.float32)
        hidden = jax.nn.silu(gate_value).astype(jnp.bfloat16)
        return stream + jnp.dot(hidden, wb_bf, preferred_element_type=jnp.float32)
    stream = lax.fori_loop(0, layer_count, apply_layer, rows_in.astype(jnp.float32))
    return stream.astype(jnp.bfloat16)

def reference(wa_local, wb_local, wa_master, wb_master, wa_moment, wb_moment, counts, inputs):
    wa_list = []
    wb_list = []
    for section_index in range(N_SECTION):
        wa_list.append(outer_update(wa_master[section_index], wa_moment[section_index], wa_local[section_index]))
        wb_list.append(outer_update(wb_master[section_index], wb_moment[section_index], wb_local[section_index]))
    wa_next = jnp.stack(wa_list)
    wb_next = jnp.stack(wb_list)
    current = inputs
    outputs = []
    for section_index in range(N_SECTION):
        current = run_section(current, counts[section_index], wa_list[section_index].astype(jnp.bfloat16), wb_list[section_index].astype(jnp.bfloat16))
        outputs.append(current)
    return (wa_next, wb_next, jnp.stack(outputs))
```

```python
import functools

import jax
import jax.numpy as jnp
from jax import lax
from jax.experimental import pallas as pl
from jax.experimental.pallas import tpu as pltpu
from jax.sharding import PartitionSpec as P


def shifted(block, axis, distance):
    devices = range(lax.axis_size(axis))
    route = [(i - distance, i) for i in devices if i - distance in devices]
    return lax.ppermute(block, axis, route)


def outer_update(master, moment, summed, replicas):
    mean_value = summed / replicas
    delta = master - mean_value
    moment_new = 0.9 * moment + delta
    return master - 0.7 * (delta + 0.9 * moment_new)


def plain_body(wa_local, wb_local, wa_master, wb_master, wa_moment, wb_moment, counts, inputs):
    replicas = lax.axis_size("replica")
    wa_summed, wb_summed = (
        lax.psum_scatter(
            wa_local[0, 0].astype(jnp.float32).astype(jnp.bfloat16),
            "replica",
            scatter_dimension=0,
            tiled=True,
        ).astype(jnp.float32),
        lax.psum_scatter(
            wb_local[0, 0].astype(jnp.float32).astype(jnp.bfloat16),
            "replica",
            scatter_dimension=1,
            tiled=True,
        ).astype(jnp.float32),
    )
    wa_next = outer_update(wa_master[0], wa_moment[0], wa_summed, replicas)
    wb_next = outer_update(wb_master[0], wb_moment[0], wb_summed, replicas)
    wa_full, wb_full = (
        lax.all_gather(wa_next.astype(jnp.bfloat16), "replica", axis=0, tiled=True),
        lax.all_gather(wb_next.astype(jnp.bfloat16), "replica", axis=1, tiled=True),
    )
    section_index = lax.axis_index("section")
    section_total = lax.axis_size("section")
    layer_count = counts[0]
    pieces = 2
    block_rows = inputs.shape[0] // pieces

    def apply_layer(step_index, stream):
        square_mean = jnp.mean(stream * stream, axis=-1, keepdims=True)
        normed = (stream * lax.rsqrt(square_mean + 1e-05)).astype(jnp.bfloat16)
        gate_value = jnp.dot(normed, wa_full, preferred_element_type=jnp.float32)
        hidden = jax.nn.silu(gate_value).astype(jnp.bfloat16)
        return stream + jnp.dot(hidden, wb_full, preferred_element_type=jnp.float32)

    def run_block(rows_in):
        stream = lax.fori_loop(0, layer_count, apply_layer, rows_in.astype(jnp.float32))
        return stream.astype(jnp.bfloat16)

    def skip_block(rows_in):
        return jnp.zeros_like(rows_in)

    def advance(step_index, incoming, output):
        offset_step = step_index - section_index
        active = jnp.logical_and(offset_step >= 0, offset_step < pieces)
        block_place = jnp.clip(offset_step, 0, pieces - 1) * block_rows
        fresh_rows = lax.dynamic_slice_in_dim(inputs, block_place, block_rows, 0)
        source = jnp.where(section_index == 0, fresh_rows, incoming)
        sent_block = lax.cond(active, run_block, skip_block, source)

        def write_block(current):
            return lax.dynamic_update_slice_in_dim(current, sent_block, block_place, 0)

        def keep_block(current):
            return current

        output = lax.cond(active, write_block, keep_block, output)
        return (sent_block, output)

    def step_body(step_index, state_pair):
        incoming, output = state_pair
        sent_block, output = advance(step_index, incoming, output)
        incoming = shifted(sent_block, "section", 1)
        return (incoming, output)

    step_count = section_total + pieces - 1
    start_rows = jnp.zeros((block_rows, inputs.shape[1]), jnp.bfloat16)
    start_output = jnp.zeros(inputs.shape, jnp.bfloat16)
    incoming, output = lax.fori_loop(0, step_count - 1, step_body, (start_rows, start_output))
    unused_block, output = advance(step_count - 1, incoming, output)
    return (wa_next[None], wb_next[None], output[None])


MESH = pl.DeviceIdType.MESH
MOST_LAYERS = 6


def fused_kernel(
    sections, pieces, cuts,
    la, lb, ma, va, mb, vb, inputs_t, counts,
    out_a, out_b, boundary_t,
    rp, sx, rx, lent, full_a, full_bt, wb_full, stream, rin, sent, held, state, fresh_buf,
    held_sem, state_sem, fresh_sem, turn,
    pair_send, pair_recv, cross_send, cross_recv,
    own_pair_send, own_pair_recv, own_cross_send, own_cross_recv,
    pass_send, pass_recv, relay_send, relay_recv,
    detour_send, detour_recv, return_send, return_recv,
):
    s = lax.axis_index("section")
    i = lax.axis_index("replica")
    core = lax.rem(i, 2)
    p = i + 1 - 2 * core
    q = lax.rem(i + 2, 4)
    pq = lax.rem(p + 2, 4)
    n = ma.shape[0]
    step = n // cuts
    tokens = rin.shape[0]
    rows = tokens // pieces
    wide = 128
    lends = s >= 2
    borrows = s + 2 < sections

    local = (lb, la)
    result = (out_b, out_a)
    full = (full_bt, full_a)

    def slice_of(owner):
        return pl.ds(pl.multiple_of(owner * n, n), n)

    loads = {}
    for t in range(2):
        for kind, owner in ((0, q), (1, i)):
            load = pltpu.make_async_copy(local[t].at[slice_of(owner)], held.at[t, kind], held_sem.at[t, kind])
            load.start()
            loads[t, kind] = load
        for which, source in enumerate(((mb, vb), (ma, va))[t]):
            load = pltpu.make_async_copy(source, state.at[t, which], state_sem.at[t, which])
            load.start()
            loads[t, 2 + which] = load

    barrier = pltpu.get_barrier_semaphore()
    pl.semaphore_signal(barrier, inc=1, device_id=(s, p), device_id_type=MESH)
    pl.semaphore_signal(barrier, inc=1, device_id=(s, q), device_id_type=MESH)

    @pl.when(s > 0)
    def _():
        pl.semaphore_signal(barrier, inc=1, device_id=(s - 1, i), device_id_type=MESH)

    @pl.when(s < sections - 1)
    def _():
        pl.semaphore_signal(barrier, inc=1, device_id=(s + 1, i), device_id_type=MESH)

    @pl.when(lends)
    def _():
        pl.semaphore_signal(barrier, inc=1, device_id=(s - 2, i), device_id_type=MESH)
        pl.semaphore_signal(barrier, inc=1, device_id=(s - 2, q), device_id_type=MESH)

    @pl.when(borrows)
    def _():
        pl.semaphore_signal(barrier, inc=1, device_id=(s + 2, i), device_id_type=MESH)
        pl.semaphore_signal(barrier, inc=1, device_id=(s + 2, q), device_id_type=MESH)

    greeted = jnp.minimum(s, 1) + jnp.minimum(sections - 1 - s, 1)
    greeted = greeted + 2 * jnp.minimum(s // 2, 1) + 2 * jnp.minimum((sections - 1 - s) // 2, 1)
    pl.semaphore_wait(barrier, 2 + greeted)

    def part(owner, k):
        return pl.ds(pl.multiple_of(owner * n + k * step, step), step)

    def remote(src, dst, send, recv, where):
        return pltpu.make_async_remote_copy(
            src_ref=src, dst_ref=dst, send_sem=send, recv_sem=recv,
            device_id=where, device_id_type=MESH,
        )

    order = [(t, k) for t in range(2) for k in range(cuts)]
    sends = []
    pair = {}
    for kind in range(2):
        for t, k in order:
            owner = pq if kind == 0 else p
            copy = remote(
                local[t].at[part(owner, k)],
                rp.at[t, kind, pl.ds(k * step, step)],
                pair_send.at[t, kind, k], pair_recv.at[t, kind, k], (s, p),
            )
            copy.start()
            pair[t, kind, k] = copy
            sends.append(copy)

    @pl.when(s == 0)
    def _():
        for block in range(tokens // wide):
            there = pl.ds(block * wide, wide)
            rin[there, :] = inputs_t[:, there].T

    def straight(k):
        return step // 3 * (2 - k % 2)

    def near(base, k):
        return pl.ds(pl.multiple_of(base + k * step, 16), straight(k))

    def far(base, k):
        return pl.ds(pl.multiple_of(base + k * step + straight(k), 16), step - straight(k))

    def ends(phase, t, rows, base):
        if phase == 0:
            return sx.at[t, rows(0, base)], rx.at[t, rows(0, base)]
        return full[t].at[rows(i * n, base)], full[t].at[rows(i * n, base)]

    def direct(phase, t, k):
        src, dst = ends(phase, t, near, k)
        send, recv = ((cross_send, cross_recv), (own_cross_send, own_cross_recv))[phase]
        return remote(src, dst, send.at[t, k], recv.at[t, k], (s, q))

    def lent_rows(phase, t, k):
        return lent.at[phase, t, k, pl.ds(0, step - straight(k))]

    def detour(phase, t, k):
        src, dst = ends(phase, t, far, k)
        return remote(
            src, lent_rows(phase, t, k), detour_send.at[phase, t, k], detour_recv.at[phase, t, k],
            (lax.rem(s + 2, sections), q),
        )

    def no_detour(phase, t, k):
        src, dst = ends(phase, t, far, k)
        return remote(src, dst, detour_send.at[phase, t, k], return_recv.at[phase, t, k], (s, q))

    def give_back(phase, t, k):
        dst = rx.at[t, far(0, k)] if phase == 0 else full[t].at[far(q * n, k)]
        return remote(
            lent_rows(phase, t, k), dst, return_send.at[phase, t, k], return_recv.at[phase, t, k],
            (lax.rem(s + sections - 2, sections), i),
        )

    def send_far(phase, t, k):
        @pl.when(borrows)
        def _():
            detour(phase, t, k).start()

        @pl.when(jnp.logical_not(borrows))
        def _():
            no_detour(phase, t, k).start()

    def send_back(phase):
        @pl.when(lends)
        def _():
            for t, k in order:
                detour(phase, t, k).wait_recv()
                give_back(phase, t, k).start()

    for t, k in order:
        if k == 0:
            loads[t, 0].wait()
        pair[t, 0, k].wait_recv()
        here = pl.ds(k * step, step)
        total = held[t, 0, here, :].astype(jnp.float32) + rp[t, 0, here, :].astype(jnp.float32)
        sx[t, here, :] = total.astype(jnp.bfloat16)
        send_far(0, t, k)

        @pl.when(jnp.logical_not(lends))
        def _():
            direct(0, t, k).start()

    send_back(0)

    @pl.when(lends)
    def _():
        for t, k in order:
            direct(0, t, k).start()

    send_back(1)

    stores = []
    own_pair = {}
    for t, k in order:
        if k == 0:
            for which in (1, 2, 3):
                loads[t, which].wait()
        pair[t, 1, k].wait_recv()
        here = pl.ds(k * step, step)
        total = held[t, 1, here, :].astype(jnp.float32) + rp[t, 1, here, :].astype(jnp.float32)
        direct(0, t, k).wait_recv()
        give_back(0, t, k).wait_recv()
        total = total + rx[t, here, :].astype(jnp.float32)
        fresh = outer_update(state[t, 0, here, :], state[t, 1, here, :], total, 4)
        fresh_buf[t, here, :] = fresh
        if k == cuts - 1:
            store = pltpu.make_async_copy(fresh_buf.at[t], result[t], fresh_sem.at[t])
            store.start()
            stores.append(store)
        mine = part(i, k)
        full[t][mine, :] = fresh.astype(jnp.bfloat16)
        send_far(1, t, k)
        direct(1, t, k).start()
        copy = remote(
            full[t].at[mine], full[t].at[mine], own_pair_send.at[t, k], own_pair_recv.at[t, k], (s, p)
        )
        copy.start()
        own_pair[t, k] = copy
        sends.append(copy)

    def collect(t):
        passed = []
        for k in range(cuts):
            direct(1, t, k).wait_recv()
            give_back(1, t, k).wait_recv()
            other = part(q, k)
            copy = remote(
                full[t].at[other], full[t].at[other], pass_send.at[t, k], pass_recv.at[t, k], (s, p)
            )
            copy.start()
            passed.append(copy)
            sends.append(copy)
        for k in range(cuts):
            own_pair[t, k].wait_recv()
            passed[k].wait_recv()

    collect(0)
    for k in range(wb_full.shape[0] // wide):
        wb_full[pl.ds(k * wide, wide), :] = full_bt[:, pl.ds(k * wide, wide)].T
    collect(1)

    layer_count = counts[0]

    def apply_layer(layer, carry):
        x = stream[...]
        scale = lax.rsqrt(jnp.mean(x * x, axis=-1, keepdims=True) + 1e-05)
        gate = jnp.dot(x.astype(jnp.bfloat16), full_a[...], preferred_element_type=jnp.float32)
        half = gate * (0.5 * scale)
        hidden = (half + half * jnp.tanh(half)).astype(jnp.bfloat16)
        change = jnp.dot(hidden, wb_full[...], preferred_element_type=jnp.float32)
        stream[...] = x + jnp.where(layer < layer_count, change, 0.0)
        return carry

    def hop(piece):
        place = pl.ds(piece * rows, rows)
        return remote(
            sent.at[place], rin.at[place], relay_send.at[piece], relay_recv.at[piece],
            (lax.rem(s + 1, sections), i),
        )

    ahead = 2
    first = jnp.logical_and(s == 0, core == 0)
    second = jnp.logical_and(s == 0, core == 1)
    for piece in range(pieces):
        place = pl.ds(piece * rows, rows)

        @pl.when(s > 0)
        def _():
            hop(piece).wait_recv()

        stream[...] = rin[place, :].astype(jnp.float32)
        if piece == 0:
            @pl.when(second)
            def _():
                pl.semaphore_wait(turn, 1)

            lax.fori_loop(0, ahead, apply_layer, 0, unroll=ahead)

            @pl.when(first)
            def _():
                pl.semaphore_signal(turn, inc=1, device_id=(s, p), device_id_type=MESH)

            lax.fori_loop(ahead, MOST_LAYERS, apply_layer, 0, unroll=MOST_LAYERS - ahead)
        else:
            lax.fori_loop(0, MOST_LAYERS, apply_layer, 0, unroll=MOST_LAYERS)
        sent[place, :] = stream[...].astype(jnp.bfloat16)

        @pl.when(s < sections - 1)
        def _():
            hop(piece).start()

        if (piece + 1) * rows % wide == 0:
            for block in range(piece * rows // wide, (piece + 1) * rows // wide):
                there = pl.ds(block * wide, wide)
                boundary_t[:, there] = sent[there, :].T

    for copy in sends:
        copy.wait_send()
    for store in stores:
        store.wait()
    for phase in range(2):
        for t, k in order:
            direct(phase, t, k).wait_send()
            no_detour(phase, t, k).wait_send()

            @pl.when(lends)
            def _():
                give_back(phase, t, k).wait_send()

    @pl.when(s < sections - 1)
    def _():
        for piece in range(pieces):
            hop(piece).wait_send()


def hand_out_kernel(parts, *refs):
    count = len(refs) // 5
    sources, results, buffers = refs[:count], refs[count : 2 * count], refs[2 * count : 3 * count]
    read_sems, write_sems = refs[3 * count : 4 * count], refs[4 * count :]
    reads = []
    for source, buffer, sem in zip(sources, buffers, read_sems):
        step = source.shape[0] // parts
        for k in range(parts):
            here = pl.ds(k * step, step)
            read = pltpu.make_async_copy(source.at[here], buffer.at[here], sem.at[k])
            read.start()
            reads.append(read)
    writes = []
    for index, (buffer, result, sem) in enumerate(zip(buffers, results, write_sems)):
        step = result.shape[0] // parts
        for k in range(parts):
            here = pl.ds(k * step, step)
            reads[index * parts + k].wait()
            write = pltpu.make_async_copy(buffer.at[here], result.at[here], sem.at[k])
            write.start()
            writes.append(write)
    for write in writes:
        write.wait()


def hand_out(*arrays):
    parts = 3
    anywhere = pl.BlockSpec(memory_space=pl.ANY)
    sems = [pltpu.SemaphoreType.DMA((parts,))] * len(arrays)
    return pl.pallas_call(
        functools.partial(hand_out_kernel, parts),
        out_shape=tuple(jax.ShapeDtypeStruct(a.shape, a.dtype) for a in arrays),
        in_specs=[anywhere] * len(arrays),
        out_specs=(anywhere,) * len(arrays),
        scratch_shapes=[pltpu.VMEM(a.shape, a.dtype) for a in arrays] + sems + sems,
    )(*arrays)


def fused_body(wa_local, wb_local, wa_master, wb_master, wa_moment, wb_moment, counts, inputs):
    sections = lax.axis_size("section")
    n, wide = wa_master.shape[1:]
    depth = wa_local.shape[2]
    tokens = inputs.shape[0]
    pieces = 2
    cuts = 3
    f32, bf16 = jnp.float32, jnp.bfloat16
    vmem = pl.BlockSpec(memory_space=pltpu.VMEM)
    anywhere = pl.BlockSpec(memory_space=pl.ANY)
    sems = pltpu.SemaphoreType.DMA
    wa_next, wb_next_t, boundary_t = pl.pallas_call(
        functools.partial(fused_kernel, sections, pieces, cuts),
        out_shape=(
            jax.ShapeDtypeStruct((n, wide), f32),
            jax.ShapeDtypeStruct((n, wide), f32),
            jax.ShapeDtypeStruct((depth, tokens), bf16),
        ),
        in_specs=[anywhere] * 6 + [vmem] + [pl.BlockSpec(memory_space=pltpu.SMEM)],
        out_specs=(anywhere, anywhere, vmem),
        scratch_shapes=[
            pltpu.VMEM((2, 2, n, wide), bf16),
            pltpu.VMEM((2, n, wide), bf16),
            pltpu.VMEM((2, n, wide), bf16),
            pltpu.VMEM((2, 2, cuts, n // cuts // 3 * 2, wide), bf16),
            pltpu.VMEM((depth, wide), bf16),
            pltpu.VMEM((depth, wide), bf16),
            pltpu.VMEM((wide, depth), bf16),
            pltpu.VMEM((tokens // pieces, depth), f32),
            pltpu.VMEM((tokens, depth), bf16),
            pltpu.VMEM((tokens, depth), bf16),
            pltpu.VMEM((2, 2, n, wide), bf16),
            pltpu.VMEM((2, 2, n, wide), f32),
            pltpu.VMEM((2, n, wide), f32),
            sems((2, 2)), sems((2, 2)), sems((2,)), pltpu.SemaphoreType.REGULAR,
            sems((2, 2, cuts)), sems((2, 2, cuts)),
            sems((2, cuts)), sems((2, cuts)),
            sems((2, cuts)), sems((2, cuts)),
            sems((2, cuts)), sems((2, cuts)),
            sems((2, cuts)), sems((2, cuts)),
            sems((pieces,)), sems((pieces,)),
            sems((2, 2, cuts)), sems((2, 2, cuts)),
            sems((2, 2, cuts)), sems((2, 2, cuts)),
        ],
        compiler_params=pltpu.CompilerParams(
            collective_id=0, has_side_effects=True, vmem_limit_bytes=56 * 1024 * 1024,
        ),
    )(
        wa_local[0, 0], wb_local[0, 0].T,
        wa_master[0], wa_moment[0], wb_master[0].T, wb_moment[0].T,
        inputs.T, counts,
    )
    wa_next, wb_next_t, boundary_t = hand_out(wa_next, wb_next_t, boundary_t)
    return (wa_next[None], wb_next_t.T[None], boundary_t.T[None])


def body(*args):
    rows = args[2].shape[1]
    if lax.axis_size("replica") == 4 and rows % 48 == 0:
        return fused_body(*args)
    return plain_body(*args)


def solution(mesh):
    return jax.shard_map(
        body,
        mesh=mesh,
        in_specs=(
            P("section", "replica", None, None),
            P("section", "replica", None, None),
            P("section", "replica", None),
            P("section", None, "replica"),
            P("section", "replica", None),
            P("section", None, "replica"),
            P("section"),
            P("replica", None),
        ),
        out_specs=(
            P("section", "replica", None),
            P("section", None, "replica"),
            P("section", "replica", None),
        ),
        check_vma=False,
    )
```

```python
import functools

import jax
import jax.numpy as jnp
from jax import lax
from jax.experimental import pallas as pl
from jax.experimental.pallas import tpu as pltpu
from jax.sharding import PartitionSpec as P


def shifted(block, axis, distance):
    devices = range(lax.axis_size(axis))
    route = [(i - distance, i) for i in devices if i - distance in devices]
    return lax.ppermute(block, axis, route)


def outer_update(master, moment, summed, replicas):
    mean_value = summed / replicas
    delta = master - mean_value
    moment_new = 0.9 * moment + delta
    return master - 0.7 * (delta + 0.9 * moment_new)


def plain_body(wa_local, wb_local, wa_master, wb_master, wa_moment, wb_moment, counts, inputs):
    replicas = lax.axis_size("replica")
    wa_summed, wb_summed = (
        lax.psum_scatter(
            wa_local[0, 0].astype(jnp.float32).astype(jnp.bfloat16),
            "replica",
            scatter_dimension=0,
            tiled=True,
        ).astype(jnp.float32),
        lax.psum_scatter(
            wb_local[0, 0].astype(jnp.float32).astype(jnp.bfloat16),
            "replica",
            scatter_dimension=1,
            tiled=True,
        ).astype(jnp.float32),
    )
    wa_next = outer_update(wa_master[0], wa_moment[0], wa_summed, replicas)
    wb_next = outer_update(wb_master[0], wb_moment[0], wb_summed, replicas)
    wa_full, wb_full = (
        lax.all_gather(wa_next.astype(jnp.bfloat16), "replica", axis=0, tiled=True),
        lax.all_gather(wb_next.astype(jnp.bfloat16), "replica", axis=1, tiled=True),
    )
    section_index = lax.axis_index("section")
    section_total = lax.axis_size("section")
    layer_count = counts[0]
    pieces = 2
    block_rows = inputs.shape[0] // pieces

    def apply_layer(step_index, stream):
        square_mean = jnp.mean(stream * stream, axis=-1, keepdims=True)
        normed = (stream * lax.rsqrt(square_mean + 1e-05)).astype(jnp.bfloat16)
        gate_value = jnp.dot(normed, wa_full, preferred_element_type=jnp.float32)
        hidden = jax.nn.silu(gate_value).astype(jnp.bfloat16)
        return stream + jnp.dot(hidden, wb_full, preferred_element_type=jnp.float32)

    def run_block(rows_in):
        stream = lax.fori_loop(0, layer_count, apply_layer, rows_in.astype(jnp.float32))
        return stream.astype(jnp.bfloat16)

    def skip_block(rows_in):
        return jnp.zeros_like(rows_in)

    def advance(step_index, incoming, output):
        offset_step = step_index - section_index
        active = jnp.logical_and(offset_step >= 0, offset_step < pieces)
        block_place = jnp.clip(offset_step, 0, pieces - 1) * block_rows
        fresh_rows = lax.dynamic_slice_in_dim(inputs, block_place, block_rows, 0)
        source = jnp.where(section_index == 0, fresh_rows, incoming)
        sent_block = lax.cond(active, run_block, skip_block, source)

        def write_block(current):
            return lax.dynamic_update_slice_in_dim(current, sent_block, block_place, 0)

        def keep_block(current):
            return current

        output = lax.cond(active, write_block, keep_block, output)
        return (sent_block, output)

    def step_body(step_index, state_pair):
        incoming, output = state_pair
        sent_block, output = advance(step_index, incoming, output)
        incoming = shifted(sent_block, "section", 1)
        return (incoming, output)

    step_count = section_total + pieces - 1
    start_rows = jnp.zeros((block_rows, inputs.shape[1]), jnp.bfloat16)
    start_output = jnp.zeros(inputs.shape, jnp.bfloat16)
    incoming, output = lax.fori_loop(0, step_count - 1, step_body, (start_rows, start_output))
    unused_block, output = advance(step_count - 1, incoming, output)
    return (wa_next[None], wb_next[None], output[None])


MESH = pl.DeviceIdType.MESH
MOST_LAYERS = 6


def fused_kernel(
    sections, pieces, cuts,
    la, lb, ma, va, mb, vb, inputs_t, counts,
    out_a, out_b, boundary_t,
    layers, lodger, rp, sx, rx, lent, full_a, full_bt, wb_full, stream, rin, sent, held, state, fresh_buf,
    held_sem, state_sem, fresh_sem,
    pair_send, pair_recv, cross_send, cross_recv,
    own_pair_send, own_pair_recv, own_cross_send, own_cross_recv,
    pass_send, pass_recv, relay_send, relay_recv,
    detour_send, detour_recv, return_send, return_recv,
    mate_send, mate_recv, share_send, share_recv, aside_send, aside_recv,
):
    s = lax.axis_index("section")
    i = lax.axis_index("replica")
    core = lax.rem(i, 2)
    p = i + 1 - 2 * core
    q = lax.rem(i + 2, 4)
    pq = lax.rem(p + 2, 4)
    n = ma.shape[0]
    step = n // cuts
    tokens = rin.shape[0]
    rows = tokens // pieces
    wide = 128
    side = lax.rem(s, 2)
    mate = s + 1 - 2 * side
    first_paired = 2 * (sections // 4)
    paired = s >= first_paired
    last = s + 2 >= sections
    patient = jnp.logical_and(s >= 2, jnp.logical_not(last))
    yields = jnp.logical_and(paired, jnp.logical_not(last))
    lends = s >= 2
    borrows = s + 2 < sections

    def borrows_at(section, k):
        some = section + 2 < sections
        if k % 2 == 0:
            some = jnp.logical_and(some, section + 4 < sections)
        return jnp.logical_and(section >= 0, some)

    local = (lb, la)
    result = (out_b, out_a)
    full = (full_bt.at[side], full_a.at[side])
    other_full = (full_bt.at[1 - side], full_a.at[1 - side])
    layers[side] = jnp.full(layers.shape[1:], counts[0]).astype(jnp.float32)

    def slice_of(owner):
        return pl.ds(pl.multiple_of(owner * n, n), n)

    loads = {}
    for t in range(2):
        for kind, owner in ((0, q), (1, i)):
            load = pltpu.make_async_copy(local[t].at[slice_of(owner)], held.at[t, kind], held_sem.at[t, kind])
            load.start()
            loads[t, kind] = load
        for which, source in enumerate(((mb, vb), (ma, va))[t]):
            load = pltpu.make_async_copy(source, state.at[t, which], state_sem.at[t, which])
            load.start()
            loads[t, 2 + which] = load

    barrier = pltpu.get_barrier_semaphore()
    pl.semaphore_signal(barrier, inc=1, device_id=(s, p), device_id_type=MESH)
    pl.semaphore_signal(barrier, inc=1, device_id=(s, q), device_id_type=MESH)

    @pl.when(s > 0)
    def _():
        pl.semaphore_signal(barrier, inc=1, device_id=(s - 1, i), device_id_type=MESH)

    @pl.when(s < sections - 1)
    def _():
        pl.semaphore_signal(barrier, inc=1, device_id=(s + 1, i), device_id_type=MESH)

    @pl.when(lends)
    def _():
        pl.semaphore_signal(barrier, inc=1, device_id=(s - 2, i), device_id_type=MESH)
        pl.semaphore_signal(barrier, inc=1, device_id=(s - 2, q), device_id_type=MESH)

    @pl.when(borrows)
    def _():
        pl.semaphore_signal(barrier, inc=1, device_id=(s + 2, i), device_id_type=MESH)
        pl.semaphore_signal(barrier, inc=1, device_id=(s + 2, q), device_id_type=MESH)

    greeted = jnp.minimum(s, 1) + jnp.minimum(sections - 1 - s, 1)
    greeted = greeted + 2 * jnp.minimum(s // 2, 1) + 2 * jnp.minimum((sections - 1 - s) // 2, 1)
    pl.semaphore_wait(barrier, 2 + greeted)

    def part(owner, k):
        return pl.ds(pl.multiple_of(owner * n + k * step, step), step)

    def remote(src, dst, send, recv, where):
        return pltpu.make_async_remote_copy(
            src_ref=src, dst_ref=dst, send_sem=send, recv_sem=recv,
            device_id=where, device_id_type=MESH,
        )

    order = [(t, k) for t in range(2) for k in range(cuts)]
    sends = []
    pair = {}
    for kind in range(2):
        for t, k in order:
            owner = pq if kind == 0 else p
            copy = remote(
                local[t].at[part(owner, k)],
                rp.at[t, kind, pl.ds(k * step, step)],
                pair_send.at[t, kind, k], pair_recv.at[t, kind, k], (s, p),
            )
            copy.start()
            pair[t, kind, k] = copy
            sends.append(copy)

    @pl.when(s == 0)
    def _():
        for block in range(tokens // wide):
            there = pl.ds(block * wide, wide)
            rin[there, :] = inputs_t[:, there].T

    def straight(k):
        return step // 3 * (2 - k % 2)

    def near(base, k):
        return pl.ds(pl.multiple_of(base + k * step, 16), straight(k))

    def far(base, k):
        return pl.ds(pl.multiple_of(base + k * step + straight(k), 16), step - straight(k))

    def ends(phase, t, rows, base):
        if phase == 0:
            return sx.at[t, rows(0, base)], rx.at[t, rows(0, base)]
        return full[t].at[rows(i * n, base)], full[t].at[rows(i * n, base)]

    def direct(phase, t, k):
        src, dst = ends(phase, t, near, k)
        send, recv = ((cross_send, cross_recv), (own_cross_send, own_cross_recv))[phase]
        return remote(src, dst, send.at[t, k], recv.at[t, k], (s, q))

    def lent_rows(phase, t, k):
        return lent.at[phase, t, k, pl.ds(0, step - straight(k))]

    def detour(phase, t, k):
        src, dst = ends(phase, t, far, k)
        return remote(
            src, lent_rows(phase, t, k), detour_send.at[phase, t, k], detour_recv.at[phase, t, k],
            (lax.rem(s + 2, sections), q),
        )

    def no_detour(phase, t, k):
        src, dst = ends(phase, t, far, k)
        return remote(src, dst, detour_send.at[phase, t, k], return_recv.at[phase, t, k], (s, q))

    def give_back(phase, t, k):
        dst = rx.at[t, far(0, k)] if phase == 0 else full[t].at[far(q * n, k)]
        return remote(
            lent_rows(phase, t, k), dst, return_send.at[phase, t, k], return_recv.at[phase, t, k],
            (lax.rem(s + sections - 2, sections), i),
        )

    def to_mate(kind, t, k):
        there = part(q if kind else i, k)
        return remote(
            full[t].at[there], full[t].at[there], mate_send.at[kind, t, k], mate_recv.at[kind, t, k], (mate, i)
        )

    def share(kind, t, k):
        there = part(q if kind else i, k)
        return remote(
            other_full[t].at[there], other_full[t].at[there],
            share_send.at[kind, t, k], share_recv.at[kind, t, k], (s, p),
        )

    def layers_aside():
        return remote(layers.at[side], layers.at[side], aside_send.at[0], aside_recv.at[0], (mate, i))

    def rows_aside(job):
        return remote(sent.at[job], lodger, aside_send.at[1], aside_recv.at[1], (mate, i))

    @pl.when(paired)
    def _():
        layers_aside().start()

    def send_far(phase, t, k):
        @pl.when(borrows_at(s, k))
        def _():
            detour(phase, t, k).start()

        @pl.when(jnp.logical_not(borrows_at(s, k)))
        def _():
            no_detour(phase, t, k).start()

    def send_back(phase, now, which=order):
        for t, k in which:
            @pl.when(jnp.logical_and(now, borrows_at(s - 2, k)))
            def _():
                detour(phase, t, k).wait_recv()
                give_back(phase, t, k).start()

    for t, k in order:
        if k == 0:
            loads[t, 0].wait()
        pair[t, 0, k].wait_recv()
        here = pl.ds(k * step, step)
        total = held[t, 0, here, :].astype(jnp.float32) + rp[t, 0, here, :].astype(jnp.float32)
        sx[t, here, :] = total.astype(jnp.bfloat16)
        send_far(0, t, k)

        @pl.when(jnp.logical_not(patient))
        def _():
            direct(0, t, k).start()

    send_back(0, lends)

    @pl.when(patient)
    def _():
        for t, k in order:
            direct(0, t, k).start()

    send_back(1, jnp.logical_not(paired))

    stores = []
    own_pair = {}
    for t, k in order:
        if k == 0:
            for which in (1, 2, 3):
                loads[t, which].wait()
        pair[t, 1, k].wait_recv()
        here = pl.ds(k * step, step)
        total = held[t, 1, here, :].astype(jnp.float32) + rp[t, 1, here, :].astype(jnp.float32)
        direct(0, t, k).wait_recv()
        give_back(0, t, k).wait_recv()
        total = total + rx[t, here, :].astype(jnp.float32)
        fresh = outer_update(state[t, 0, here, :], state[t, 1, here, :], total, 4)
        fresh_buf[t, here, :] = fresh
        if k == cuts - 1:
            store = pltpu.make_async_copy(fresh_buf.at[t], result[t], fresh_sem.at[t])
            store.start()
            stores.append(store)
        mine = part(i, k)
        full[t][mine, :] = fresh.astype(jnp.bfloat16)
        send_far(1, t, k)

        @pl.when(jnp.logical_not(yields))
        def _():
            direct(1, t, k).start()

        copy = remote(
            full[t].at[mine], full[t].at[mine], own_pair_send.at[t, k], own_pair_recv.at[t, k], (s, p)
        )
        copy.start()
        own_pair[t, k] = copy
        sends.append(copy)

        @pl.when(paired)
        def _():
            to_mate(0, t, k).start()

        send_back(1, paired, [(t, k)])

    @pl.when(yields)
    def _():
        for t, k in order:
            direct(1, t, k).start()

    def collect(t):
        passed = []
        for k in range(cuts):
            direct(1, t, k).wait_recv()
            give_back(1, t, k).wait_recv()
            other = part(q, k)
            copy = remote(
                full[t].at[other], full[t].at[other], pass_send.at[t, k], pass_recv.at[t, k], (s, p)
            )
            copy.start()
            passed.append(copy)
            sends.append(copy)

            @pl.when(paired)
            def _():
                to_mate(1, t, k).start()

        for k in range(cuts):
            own_pair[t, k].wait_recv()
            passed[k].wait_recv()

    def turn_over(slot):
        for k in range(wb_full.shape[1] // wide):
            there = pl.ds(k * wide, wide)
            wb_full[slot, there, :] = full_bt[slot, :, there].T

    collect(0)
    turn_over(side)
    collect(1)

    def take_in(kind):
        for t, k in order:
            to_mate(kind, t, k).wait_recv()
            share(kind, t, k).start()

    def take_in_rest():
        take_in(1)
        for t in range(2):
            for kind in range(2):
                for k in range(cuts):
                    share(kind, t, k).wait_recv()
            if t == 0:
                turn_over(1 - side)
        layers_aside().wait_recv()

    @pl.when(paired)
    def _():
        take_in(0)

    late = jnp.logical_and(yields, side == 0)

    @pl.when(jnp.logical_and(paired, jnp.logical_not(late)))
    def _():
        take_in_rest()

    def piece_at(piece):
        return pl.ds(pl.multiple_of(piece * rows, rows), rows)

    def hop(job, piece, there):
        return remote(
            sent.at[job], rin.at[piece_at(piece)], relay_send.at[job], relay_recv.at[piece],
            (lax.rem(there, sections), i),
        )

    for job in range(2):
        piece = jnp.where(paired, side, job)
        slot = jnp.where(paired, job, side)
        stays = jnp.logical_and(paired, job == 1)

        if job == 1:
            @pl.when(late)
            def _():
                take_in_rest()

        @pl.when(jnp.logical_and(s > 0, jnp.logical_not(stays)))
        def _():
            hop(job, piece, s).wait_recv()

        @pl.when(stays)
        def _():
            stream[...] = sent[0].astype(jnp.float32)

        @pl.when(jnp.logical_not(stays))
        def _():
            stream[...] = rin[piece_at(piece), :].astype(jnp.float32)

        def apply_layer(layer, carry):
            x = stream[...]
            scale = lax.rsqrt(jnp.mean(x * x, axis=-1, keepdims=True) + 1e-05)
            gate = jnp.dot(x.astype(jnp.bfloat16), full_a[slot], preferred_element_type=jnp.float32)
            half = gate * (0.5 * scale)
            hidden = (half + half * jnp.tanh(half)).astype(jnp.bfloat16)
            change = jnp.dot(hidden, wb_full[slot], preferred_element_type=jnp.float32)
            active = jnp.broadcast_to(layers[slot, 0:1, 0:1], change.shape) > layer
            stream[...] = x + jnp.where(active, change, 0.0)
            return carry

        lax.fori_loop(0, MOST_LAYERS, apply_layer, 0, unroll=MOST_LAYERS)
        sent[job] = stream[...].astype(jnp.bfloat16)

        if job == 1:
            @pl.when(jnp.logical_and(paired, s + 2 < sections))
            def _():
                hop(job, piece, s + 2).start()

        @pl.when(jnp.logical_not(paired))
        def _():
            hop(job, piece, s + 1 + job * (s + 1 == first_paired)).start()

        @pl.when(jnp.logical_and(paired, side != job))
        def _():
            rows_aside(job).start()

        @pl.when(jnp.logical_not(jnp.logical_and(paired, side != job)))
        def _():
            boundary_t[:, piece_at(piece)] = sent[job].T

    @pl.when(paired)
    def _():
        rows_aside(0).wait_recv()
        boundary_t[:, piece_at(1 - side)] = lodger[...].T

    for copy in sends:
        copy.wait_send()
    for store in stores:
        store.wait()
    for phase in range(2):
        for t, k in order:
            direct(phase, t, k).wait_send()
            no_detour(phase, t, k).wait_send()

            @pl.when(borrows_at(s - 2, k))
            def _():
                give_back(phase, t, k).wait_send()

    @pl.when(jnp.logical_not(paired))
    def _():
        hop(0, 0, s).wait_send()

    @pl.when(jnp.logical_or(jnp.logical_not(paired), s + 2 < sections))
    def _():
        hop(1, 0, s).wait_send()

    @pl.when(paired)
    def _():
        rows_aside(0).wait_send()
        layers_aside().wait_send()
        for kind in range(2):
            for t, k in order:
                to_mate(kind, t, k).wait_send()
                share(kind, t, k).wait_send()


def hand_out_kernel(parts, *refs):
    count = len(refs) // 5
    sources, results, buffers = refs[:count], refs[count : 2 * count], refs[2 * count : 3 * count]
    read_sems, write_sems = refs[3 * count : 4 * count], refs[4 * count :]
    reads = []
    for source, buffer, sem in zip(sources, buffers, read_sems):
        step = source.shape[0] // parts
        for k in range(parts):
            here = pl.ds(k * step, step)
            read = pltpu.make_async_copy(source.at[here], buffer.at[here], sem.at[k])
            read.start()
            reads.append(read)
    writes = []
    for index, (buffer, result, sem) in enumerate(zip(buffers, results, write_sems)):
        step = result.shape[0] // parts
        for k in range(parts):
            here = pl.ds(k * step, step)
            reads[index * parts + k].wait()
            write = pltpu.make_async_copy(buffer.at[here], result.at[here], sem.at[k])
            write.start()
            writes.append(write)
    for write in writes:
        write.wait()


def hand_out(*arrays):
    parts = 3
    anywhere = pl.BlockSpec(memory_space=pl.ANY)
    sems = [pltpu.SemaphoreType.DMA((parts,))] * len(arrays)
    return pl.pallas_call(
        functools.partial(hand_out_kernel, parts),
        out_shape=tuple(jax.ShapeDtypeStruct(a.shape, a.dtype) for a in arrays),
        in_specs=[anywhere] * len(arrays),
        out_specs=(anywhere,) * len(arrays),
        scratch_shapes=[pltpu.VMEM(a.shape, a.dtype) for a in arrays] + sems + sems,
    )(*arrays)


def fused_body(wa_local, wb_local, wa_master, wb_master, wa_moment, wb_moment, counts, inputs):
    sections = lax.axis_size("section")
    n, wide = wa_master.shape[1:]
    depth = wa_local.shape[2]
    tokens = inputs.shape[0]
    pieces = 2
    cuts = 3
    f32, bf16 = jnp.float32, jnp.bfloat16
    vmem = pl.BlockSpec(memory_space=pltpu.VMEM)
    anywhere = pl.BlockSpec(memory_space=pl.ANY)
    sems = pltpu.SemaphoreType.DMA
    wa_next, wb_next_t, boundary_t = pl.pallas_call(
        functools.partial(fused_kernel, sections, pieces, cuts),
        out_shape=(
            jax.ShapeDtypeStruct((n, wide), f32),
            jax.ShapeDtypeStruct((n, wide), f32),
            jax.ShapeDtypeStruct((depth, tokens), bf16),
        ),
        in_specs=[anywhere] * 6 + [vmem] + [pl.BlockSpec(memory_space=pltpu.SMEM)],
        out_specs=(anywhere, anywhere, vmem),
        scratch_shapes=[
            pltpu.VMEM((2, 8, 128), f32),
            pltpu.VMEM((tokens // pieces, depth), bf16),
            pltpu.VMEM((2, 2, n, wide), bf16),
            pltpu.VMEM((2, n, wide), bf16),
            pltpu.VMEM((2, n, wide), bf16),
            pltpu.VMEM((2, 2, cuts, n // cuts // 3 * 2, wide), bf16),
            pltpu.VMEM((2, depth, wide), bf16),
            pltpu.VMEM((2, depth, wide), bf16),
            pltpu.VMEM((2, wide, depth), bf16),
            pltpu.VMEM((tokens // pieces, depth), f32),
            pltpu.VMEM((tokens, depth), bf16),
            pltpu.VMEM((pieces, tokens // pieces, depth), bf16),
            pltpu.VMEM((2, 2, n, wide), bf16),
            pltpu.VMEM((2, 2, n, wide), f32),
            pltpu.VMEM((2, n, wide), f32),
            sems((2, 2)), sems((2, 2)), sems((2,)),
            sems((2, 2, cuts)), sems((2, 2, cuts)),
            sems((2, cuts)), sems((2, cuts)),
            sems((2, cuts)), sems((2, cuts)),
            sems((2, cuts)), sems((2, cuts)),
            sems((2, cuts)), sems((2, cuts)),
            sems((pieces,)), sems((pieces,)),
            sems((2, 2, cuts)), sems((2, 2, cuts)),
            sems((2, 2, cuts)), sems((2, 2, cuts)),
            sems((2, 2, cuts)), sems((2, 2, cuts)),
            sems((2, 2, cuts)), sems((2, 2, cuts)),
            sems((2,)), sems((2,)),
        ],
        compiler_params=pltpu.CompilerParams(
            collective_id=0, has_side_effects=True, vmem_limit_bytes=56 * 1024 * 1024,
        ),
    )(
        wa_local[0, 0], wb_local[0, 0].T,
        wa_master[0], wa_moment[0], wb_master[0].T, wb_moment[0].T,
        inputs.T, counts,
    )
    wa_next, wb_next_t, boundary_t = hand_out(wa_next, wb_next_t, boundary_t)
    return (wa_next[None], wb_next_t.T[None], boundary_t.T[None])


def body(*args):
    rows = args[2].shape[1]
    sections = lax.axis_size("section")
    tokens = args[7].shape[0]
    if lax.axis_size("replica") == 4 and sections % 2 == 0 and sections >= 4 and rows % 144 == 0 and tokens % 256 == 0:
        return fused_body(*args)
    return plain_body(*args)


def solution(mesh):
    return jax.shard_map(
        body,
        mesh=mesh,
        in_specs=(
            P("section", "replica", None, None),
            P("section", "replica", None, None),
            P("section", "replica", None),
            P("section", None, "replica"),
            P("section", "replica", None),
            P("section", None, "replica"),
            P("section"),
            P("replica", None),
        ),
        out_specs=(
            P("section", "replica", None),
            P("section", None, "replica"),
            P("section", "replica", None),
        ),
        check_vma=False,
    )
```

```python
import functools

import jax
import jax.numpy as jnp
from jax import lax
from jax.experimental import pallas as pl
from jax.experimental.pallas import tpu as pltpu
from jax.sharding import PartitionSpec as P


def shifted(block, axis, distance):
    devices = range(lax.axis_size(axis))
    route = [(i - distance, i) for i in devices if i - distance in devices]
    return lax.ppermute(block, axis, route)


def outer_update(master, moment, summed, replicas):
    mean_value = summed / replicas
    delta = master - mean_value
    moment_new = 0.9 * moment + delta
    return master - 0.7 * (delta + 0.9 * moment_new)


def plain_body(wa_local, wb_local, wa_master, wb_master, wa_moment, wb_moment, counts, inputs):
    replicas = lax.axis_size("replica")
    wa_summed, wb_summed = (
        lax.psum_scatter(
            wa_local[0, 0].astype(jnp.float32).astype(jnp.bfloat16),
            "replica",
            scatter_dimension=0,
            tiled=True,
        ).astype(jnp.float32),
        lax.psum_scatter(
            wb_local[0, 0].astype(jnp.float32).astype(jnp.bfloat16),
            "replica",
            scatter_dimension=1,
            tiled=True,
        ).astype(jnp.float32),
    )
    wa_next = outer_update(wa_master[0], wa_moment[0], wa_summed, replicas)
    wb_next = outer_update(wb_master[0], wb_moment[0], wb_summed, replicas)
    wa_full, wb_full = (
        lax.all_gather(wa_next.astype(jnp.bfloat16), "replica", axis=0, tiled=True),
        lax.all_gather(wb_next.astype(jnp.bfloat16), "replica", axis=1, tiled=True),
    )
    section_index = lax.axis_index("section")
    section_total = lax.axis_size("section")
    layer_count = counts[0]
    pieces = 2
    block_rows = inputs.shape[0] // pieces

    def apply_layer(step_index, stream):
        square_mean = jnp.mean(stream * stream, axis=-1, keepdims=True)
        normed = (stream * lax.rsqrt(square_mean + 1e-05)).astype(jnp.bfloat16)
        gate_value = jnp.dot(normed, wa_full, preferred_element_type=jnp.float32)
        hidden = jax.nn.silu(gate_value).astype(jnp.bfloat16)
        return stream + jnp.dot(hidden, wb_full, preferred_element_type=jnp.float32)

    def run_block(rows_in):
        stream = lax.fori_loop(0, layer_count, apply_layer, rows_in.astype(jnp.float32))
        return stream.astype(jnp.bfloat16)

    def skip_block(rows_in):
        return jnp.zeros_like(rows_in)

    def advance(step_index, incoming, output):
        offset_step = step_index - section_index
        active = jnp.logical_and(offset_step >= 0, offset_step < pieces)
        block_place = jnp.clip(offset_step, 0, pieces - 1) * block_rows
        fresh_rows = lax.dynamic_slice_in_dim(inputs, block_place, block_rows, 0)
        source = jnp.where(section_index == 0, fresh_rows, incoming)
        sent_block = lax.cond(active, run_block, skip_block, source)

        def write_block(current):
            return lax.dynamic_update_slice_in_dim(current, sent_block, block_place, 0)

        def keep_block(current):
            return current

        output = lax.cond(active, write_block, keep_block, output)
        return (sent_block, output)

    def step_body(step_index, state_pair):
        incoming, output = state_pair
        sent_block, output = advance(step_index, incoming, output)
        incoming = shifted(sent_block, "section", 1)
        return (incoming, output)

    step_count = section_total + pieces - 1
    start_rows = jnp.zeros((block_rows, inputs.shape[1]), jnp.bfloat16)
    start_output = jnp.zeros(inputs.shape, jnp.bfloat16)
    incoming, output = lax.fori_loop(0, step_count - 1, step_body, (start_rows, start_output))
    unused_block, output = advance(step_count - 1, incoming, output)
    return (wa_next[None], wb_next[None], output[None])


MESH = pl.DeviceIdType.MESH
MOST_LAYERS = 6


def fused_kernel(
    sections, pieces, cuts,
    la, lb, ma, va, mb, vb, inputs_t, counts,
    out_a, out_b, boundary_t,
    own_layers, inputs_here, layers, lodger, rp, sx, rx, lent, full_a, full_bt, wb_full, stream, rin, sent, held, state,
    held_sem, state_sem, small_sem,
    pair_send, pair_recv, own_pair_send, own_pair_recv,
    pass_send, pass_recv, relay_send, relay_recv,
    y_send, y_recv, lent_recv, back_send,
    mate_send, mate_recv, share_send, share_recv, aside_send, aside_recv,
):
    s = lax.axis_index("section")
    i = lax.axis_index("replica")
    core = lax.rem(i, 2)
    p = i + 1 - 2 * core
    q = lax.rem(i + 2, 4)
    pq = lax.rem(p + 2, 4)
    n = ma.shape[0]
    step = n // cuts
    tokens = rin.shape[0]
    rows = tokens // pieces
    wide = 128
    side = lax.rem(s, 2)
    mate = s + 1 - 2 * side
    first_paired = 2 * (sections // 4)
    paired = s >= first_paired
    last = s + 2 >= sections
    patient = jnp.logical_and(s >= 2, jnp.logical_not(last))
    yields = jnp.logical_and(paired, jnp.logical_not(last))
    lends = s >= 2
    borrows = s + 2 < sections
    interleaves = jnp.logical_or(paired, s == 1)

    def middle(section):
        return jnp.logical_and(section >= 2, section < first_paired)

    def over_z(section, share, phase):
        some = jnp.logical_and(section >= 0, section + 2 < sections)
        if share == 0 and phase == 1:
            return section < -sections
        if share == 0:
            return jnp.logical_and(some, middle(section))
        if phase == 1:
            return some
        return jnp.logical_and(some, jnp.logical_not(middle(section)))

    def over_x(section, share, k):
        return section == 0 if share == 0 and k == 0 else None

    local = (lb, la)
    result = (out_b, out_a)
    full = (full_bt.at[side], full_a.at[side])
    other_full = (full_bt.at[1 - side], full_a.at[1 - side])

    def slice_of(owner):
        return pl.ds(pl.multiple_of(owner * n, n), n)

    barrier = pltpu.get_barrier_semaphore()
    pl.semaphore_signal(barrier, inc=1, device_id=(s, p), device_id_type=MESH)
    pl.semaphore_signal(barrier, inc=1, device_id=(s, q), device_id_type=MESH)

    @pl.when(s > 0)
    def _():
        pl.semaphore_signal(barrier, inc=1, device_id=(s - 1, i), device_id_type=MESH)

    @pl.when(s < sections - 1)
    def _():
        pl.semaphore_signal(barrier, inc=1, device_id=(s + 1, i), device_id_type=MESH)

    @pl.when(lends)
    def _():
        pl.semaphore_signal(barrier, inc=1, device_id=(s - 2, i), device_id_type=MESH)
        pl.semaphore_signal(barrier, inc=1, device_id=(s - 2, q), device_id_type=MESH)

    @pl.when(borrows)
    def _():
        pl.semaphore_signal(barrier, inc=1, device_id=(s + 2, i), device_id_type=MESH)
        pl.semaphore_signal(barrier, inc=1, device_id=(s + 2, q), device_id_type=MESH)

    @pl.when(s < 2)
    def _():
        pl.semaphore_signal(barrier, inc=1, device_id=(1 - s, q), device_id_type=MESH)

    loads = {}
    for kind, owner in ((0, q), (1, i)):
        for t in range(2):
            load = pltpu.make_async_copy(local[t].at[slice_of(owner)], held.at[t, kind], held_sem.at[t, kind])
            load.start()
            loads[t, kind] = load

    layers_load = pltpu.make_async_copy(counts, own_layers, small_sem.at[0])
    layers_load.start()
    inputs_load = pltpu.make_async_copy(inputs_t, inputs_here, small_sem.at[1])

    @pl.when(s == 0)
    def _():
        inputs_load.start()

    greeted = jnp.maximum(2 - s, 0) - jnp.maximum(1 - s, 0) + jnp.minimum(s, 1) + jnp.minimum(sections - 1 - s, 1)
    greeted = greeted + 2 * jnp.minimum(s // 2, 1) + 2 * jnp.minimum((sections - 1 - s) // 2, 1)
    pl.semaphore_wait(barrier, 2 + greeted)

    def part(owner, k):
        return pl.ds(pl.multiple_of(owner * n + k * step, step), step)

    def remote(src, dst, send, recv, where):
        return pltpu.make_async_remote_copy(
            src_ref=src, dst_ref=dst, send_sem=send, recv_sem=recv,
            device_id=where, device_id_type=MESH,
        )

    order = [(t, k) for t in range(2) for k in range(cuts)]
    sends = []
    pair = {}
    for kind in range(2):
        for t, k in order:
            owner = pq if kind == 0 else p
            copy = remote(
                local[t].at[part(owner, k)],
                rp.at[t, kind, pl.ds(k * step, step)],
                pair_send.at[t, kind, k], pair_recv.at[t, kind, k], (s, p),
            )
            copy.start()
            pair[t, kind, k] = copy
            sends.append(copy)

    for t in range(2):
        for which, source in enumerate(((mb, vb), (ma, va))[t]):
            load = pltpu.make_async_copy(source, state.at[t, which], state_sem.at[t, which])
            load.start()
            loads[t, 2 + which] = load

    @pl.when(s == 0)
    def _():
        inputs_load.wait()
        for block in range(tokens // wide):
            there = pl.ds(block * wide, wide)
            rin[there, :] = inputs_here[:, there].T

    def portion(share, k):
        first = step // 3 * min(k + 1, 2)
        return (0, first) if share == 0 else (first, step - first)

    def share_rows(base, share, k):
        start, size = portion(share, k)
        return pl.ds(pl.multiple_of(base + k * step + start, 16), size)

    def ends(phase, share, t, k):
        if phase == 0:
            return sx.at[t, share_rows(0, share, k)], rx.at[t, share_rows(0, share, k)]
        there = full[t].at[share_rows(i * n, share, k)]
        return there, there

    def direct(phase, share, t, k):
        src, dst = ends(phase, share, t, k)
        return remote(src, dst, y_send.at[phase, share, t, k], y_recv.at[phase, share, t, k], (s, q))

    def lent_rows(phase, share, t, k):
        start, size = portion(share, k)
        return lent.at[phase, t, k, pl.ds(start, size)]

    def detour(phase, share, t, k, stride):
        src, dst = ends(phase, share, t, k)
        return remote(
            src, lent_rows(phase, share, t, k), y_send.at[phase, share, t, k], lent_recv.at[phase, share, t, k],
            (lax.rem(s + stride, sections), q),
        )

    def give_back(phase, share, t, k, stride):
        base = 0 if phase == 0 else q * n
        there = other_full[t] if stride == 1 else full[t]
        dst = (rx.at[t] if phase == 0 else there).at[share_rows(base, share, k)]
        return remote(
            lent_rows(phase, share, t, k), dst, back_send.at[phase, share, t, k], y_recv.at[phase, share, t, k],
            (lax.rem(s + sections - stride, sections), i),
        )

    def send_detours(phase, t, k):
        for share in range(2):
            @pl.when(over_z(s, share, phase))
            def _():
                detour(phase, share, t, k, 2).start()

            sideways = over_x(s, share, k)
            if sideways is not None:
                @pl.when(sideways)
                def _():
                    detour(phase, share, t, k, 1).start()

    def send_direct(phase, t, k, now):
        for share in range(2):
            stays_here = jnp.logical_not(over_z(s, share, phase))
            sideways = over_x(s, share, k)
            if sideways is not None:
                stays_here = jnp.logical_and(stays_here, jnp.logical_not(sideways))

            @pl.when(jnp.logical_and(now, stays_here))
            def _():
                direct(phase, share, t, k).start()

    def each_lent(phase, t, k, act):
        for share in range(2):
            @pl.when(over_z(s - 2, share, phase))
            def _():
                act(share, 2)

            sideways = over_x(s - 1, share, k)
            if sideways is not None:
                @pl.when(sideways)
                def _():
                    act(share, 1)

    def send_back(phase, now, which):
        for t, k in which:
            @pl.when(now)
            def _():
                def act(share, stride):
                    detour(phase, share, t, k, stride).wait_recv()
                    give_back(phase, share, t, k, stride).start()

                each_lent(phase, t, k, act)

    def to_mate(kind, t, k):
        there = part(q if kind else i, k)
        return remote(
            full[t].at[there], full[t].at[there], mate_send.at[kind, t, k], mate_recv.at[kind, t, k], (mate, i)
        )

    def to_partner(kind, t, k):
        there = part(q if kind else i, k)
        return remote(
            other_full[t].at[there], other_full[t].at[there],
            share_send.at[kind, t, k], share_recv.at[kind, t, k], (s, p),
        )

    def layers_aside():
        return remote(layers.at[side], layers.at[side], aside_send.at[0], aside_recv.at[0], (mate, i))

    def rows_aside(job):
        return remote(sent.at[job], lodger, aside_send.at[1], aside_recv.at[1], (mate, i))

    layers_load.wait()
    layers[side] = jnp.full(layers.shape[1:], own_layers[0]).astype(jnp.float32)

    @pl.when(paired)
    def _():
        layers_aside().start()

    for t, k in order:
        if k == 0:
            loads[t, 0].wait()
        pair[t, 0, k].wait_recv()
        here = pl.ds(k * step, step)
        total = held[t, 0, here, :].astype(jnp.float32) + rp[t, 0, here, :].astype(jnp.float32)
        sx[t, here, :] = total.astype(jnp.bfloat16)
        send_detours(0, t, k)
        send_direct(0, t, k, jnp.logical_not(patient))

    send_back(0, s >= 1, order)
    for t, k in order:
        send_direct(0, t, k, patient)
    send_back(1, jnp.logical_not(interleaves), order)

    lag = 2
    own_pair = {}
    for t, k in order:
        if k == 0:
            for which in (1, 2, 3):
                loads[t, which].wait()
        pair[t, 1, k].wait_recv()
        here = pl.ds(k * step, step)
        total = held[t, 1, here, :].astype(jnp.float32) + rp[t, 1, here, :].astype(jnp.float32)
        for share in range(2):
            direct(0, share, t, k).wait_recv()
        total = total + rx[t, here, :].astype(jnp.float32)
        fresh = outer_update(state[t, 0, here, :], state[t, 1, here, :], total, 4)
        result[t][here, :] = fresh
        mine = part(i, k)
        full[t][mine, :] = fresh.astype(jnp.bfloat16)
        send_detours(1, t, k)
        send_direct(1, t, k, True)
        copy = remote(
            full[t].at[mine], full[t].at[mine], own_pair_send.at[t, k], own_pair_recv.at[t, k], (s, p)
        )
        copy.start()
        own_pair[t, k] = copy
        sends.append(copy)

        @pl.when(paired)
        def _():
            to_mate(0, t, k).start()

        send_back(1, s == 1, [(t, k)])
        done = order.index((t, k)) + 1 - lag
        if done > 0:
            send_back(1, paired, [order[done - 1]])

    send_back(1, paired, order[len(order) - lag :])

    def collect(t):
        passed = []
        for k in range(cuts):
            for share in range(2):
                direct(1, share, t, k).wait_recv()
            other = part(q, k)
            copy = remote(
                full[t].at[other], full[t].at[other], pass_send.at[t, k], pass_recv.at[t, k], (s, p)
            )
            copy.start()
            passed.append(copy)
            sends.append(copy)

            @pl.when(paired)
            def _():
                to_mate(1, t, k).start()

        for k in range(cuts):
            own_pair[t, k].wait_recv()
            passed[k].wait_recv()

    def turn_over(slot):
        for k in range(wb_full.shape[1] // wide):
            there = pl.ds(k * wide, wide)
            wb_full[slot, there, :] = full_bt[slot, :, there].T

    collect(0)
    turn_over(side)
    collect(1)

    def take_in(kind, t):
        for k in range(cuts):
            to_mate(kind, t, k).wait_recv()
            to_partner(kind, t, k).start()

    def take_in_rest(t):
        take_in(1, t)
        for kind in range(2):
            for k in range(cuts):
                to_partner(kind, t, k).wait_recv()

    @pl.when(paired)
    def _():
        take_in(0, 0)
        take_in(0, 1)
        take_in_rest(0)
        turn_over(1 - side)
        layers_aside().wait_recv()

    late = jnp.logical_and(yields, side == 0)

    @pl.when(jnp.logical_and(paired, jnp.logical_not(late)))
    def _():
        take_in_rest(1)

    def piece_at(piece):
        return pl.ds(pl.multiple_of(piece * rows, rows), rows)

    def hop(job, piece, there):
        return remote(
            sent.at[job], rin.at[piece_at(piece)], relay_send.at[job], relay_recv.at[piece],
            (lax.rem(there, sections), i),
        )

    for job in range(2):
        piece = jnp.where(paired, side, job)
        slot = jnp.where(paired, job, side)
        stays = jnp.logical_and(paired, job == 1)

        if job == 1:
            @pl.when(late)
            def _():
                take_in_rest(1)

        @pl.when(jnp.logical_and(s > 0, jnp.logical_not(stays)))
        def _():
            hop(job, piece, s).wait_recv()

        @pl.when(stays)
        def _():
            stream[...] = sent[0].astype(jnp.float32)

        @pl.when(jnp.logical_not(stays))
        def _():
            stream[...] = rin[piece_at(piece), :].astype(jnp.float32)

        def apply_layer(layer, carry):
            x = stream[...]
            scale = lax.rsqrt(jnp.mean(x * x, axis=-1, keepdims=True) + 1e-05)
            gate = jnp.dot(x.astype(jnp.bfloat16), full_a[slot], preferred_element_type=jnp.float32)
            half = gate * (0.5 * scale)
            hidden = (half + half * jnp.tanh(half)).astype(jnp.bfloat16)
            change = jnp.dot(hidden, wb_full[slot], preferred_element_type=jnp.float32)
            active = jnp.broadcast_to(layers[slot, 0:1, 0:1], change.shape) > layer
            stream[...] = x + jnp.where(active, change, 0.0)
            return carry

        lax.fori_loop(0, MOST_LAYERS, apply_layer, 0, unroll=MOST_LAYERS)
        sent[job] = stream[...].astype(jnp.bfloat16)

        if job == 1:
            @pl.when(jnp.logical_and(paired, s + 2 < sections))
            def _():
                hop(job, piece, s + 2).start()

        @pl.when(jnp.logical_not(paired))
        def _():
            hop(job, piece, s + 1 + job * (s + 1 == first_paired)).start()

        @pl.when(jnp.logical_and(paired, side != job))
        def _():
            rows_aside(job).start()

    @pl.when(jnp.logical_not(paired))
    def _():
        boundary_t[:, piece_at(0)] = sent[0].T
        boundary_t[:, piece_at(1)] = sent[1].T

    @pl.when(paired)
    def _():
        boundary_t[:, piece_at(side)] = sent[side].T
        rows_aside(0).wait_recv()
        boundary_t[:, piece_at(1 - side)] = lodger[...].T

    for copy in sends:
        copy.wait_send()
    for phase in range(2):
        for t, k in order:
            for share in range(2):
                direct(phase, share, t, k).wait_send()

            def act(share, stride):
                give_back(phase, share, t, k, stride).wait_send()

            each_lent(phase, t, k, act)

    @pl.when(jnp.logical_not(paired))
    def _():
        hop(0, 0, s).wait_send()

    @pl.when(jnp.logical_or(jnp.logical_not(paired), s + 2 < sections))
    def _():
        hop(1, 0, s).wait_send()

    @pl.when(paired)
    def _():
        rows_aside(0).wait_send()
        layers_aside().wait_send()
        for kind in range(2):
            for t, k in order:
                to_mate(kind, t, k).wait_send()
                to_partner(kind, t, k).wait_send()


def hand_out_kernel(parts, *refs):
    count = len(refs) // 3
    writes = []
    for source, result, sem in zip(refs[:count], refs[count : 2 * count], refs[2 * count :]):
        step = result.shape[0] // parts
        for k in range(parts):
            here = pl.ds(k * step, step)
            write = pltpu.make_async_copy(source.at[here], result.at[here], sem.at[k])
            write.start()
            writes.append(write)
    for write in writes:
        write.wait()


def hand_out(*arrays):
    parts = 3
    return pl.pallas_call(
        functools.partial(hand_out_kernel, parts),
        out_shape=tuple(jax.ShapeDtypeStruct(a.shape, a.dtype) for a in arrays),
        in_specs=[pl.BlockSpec(memory_space=pl.ANY)] * len(arrays),
        out_specs=(pl.BlockSpec(memory_space=pl.ANY),) * len(arrays),
        scratch_shapes=[pltpu.SemaphoreType.DMA((parts,))] * len(arrays),
    )(*(pltpu.with_memory_space_constraint(a, pltpu.VMEM) for a in arrays))


def fused_body(wa_local, wb_local, wa_master, wb_master, wa_moment, wb_moment, counts, inputs):
    sections = lax.axis_size("section")
    n, wide = wa_master.shape[1:]
    depth = wa_local.shape[2]
    tokens = inputs.shape[0]
    pieces = 2
    cuts = 3
    f32, bf16 = jnp.float32, jnp.bfloat16
    vmem = pl.BlockSpec(memory_space=pltpu.VMEM)
    anywhere = pl.BlockSpec(memory_space=pl.ANY)
    sems = pltpu.SemaphoreType.DMA
    wa_next, wb_next_t, boundary_t = pl.pallas_call(
        functools.partial(fused_kernel, sections, pieces, cuts),
        out_shape=(
            pltpu.VMEM((n, wide), f32),
            pltpu.VMEM((n, wide), f32),
            pltpu.VMEM((depth, tokens), bf16),
        ),
        in_specs=[anywhere] * 8,
        out_specs=(vmem, vmem, vmem),
        scratch_shapes=[
            pltpu.SMEM((1,), jnp.int32),
            pltpu.VMEM((depth, tokens), bf16),
            pltpu.VMEM((2, 8, 128), f32),
            pltpu.VMEM((tokens // pieces, depth), bf16),
            pltpu.VMEM((2, 2, n, wide), bf16),
            pltpu.VMEM((2, n, wide), bf16),
            pltpu.VMEM((2, n, wide), bf16),
            pltpu.VMEM((2, 2, cuts, n // cuts, wide), bf16),
            pltpu.VMEM((2, depth, wide), bf16),
            pltpu.VMEM((2, depth, wide), bf16),
            pltpu.VMEM((2, wide, depth), bf16),
            pltpu.VMEM((tokens // pieces, depth), f32),
            pltpu.VMEM((tokens, depth), bf16),
            pltpu.VMEM((pieces, tokens // pieces, depth), bf16),
            pltpu.VMEM((2, 2, n, wide), bf16),
            pltpu.VMEM((2, 2, n, wide), f32),
            sems((2, 2)), sems((2, 2)), sems((2,)),
            sems((2, 2, cuts)), sems((2, 2, cuts)),
            sems((2, cuts)), sems((2, cuts)),
            sems((2, cuts)), sems((2, cuts)),
            sems((pieces,)), sems((pieces,)),
            sems((2, 2, 2, cuts)), sems((2, 2, 2, cuts)),
            sems((2, 2, 2, cuts)), sems((2, 2, 2, cuts)),
            sems((2, 2, cuts)), sems((2, 2, cuts)),
            sems((2, 2, cuts)), sems((2, 2, cuts)),
            sems((2,)), sems((2,)),
        ],
        compiler_params=pltpu.CompilerParams(
            collective_id=0, has_side_effects=True, vmem_limit_bytes=56 * 1024 * 1024,
        ),
    )(
        wa_local[0, 0], wb_local[0, 0].T,
        wa_master[0], wa_moment[0], wb_master[0].T, wb_moment[0].T,
        inputs.T, counts,
    )
    wa_next, wb_next_t, boundary_t = hand_out(wa_next, wb_next_t, boundary_t)
    return (wa_next[None], wb_next_t.T[None], boundary_t.T[None])


def body(*args):
    rows = args[2].shape[1]
    sections = lax.axis_size("section")
    tokens = args[7].shape[0]
    if lax.axis_size("replica") == 4 and sections % 2 == 0 and sections >= 4 and rows % 144 == 0 and tokens % 256 == 0:
        return fused_body(*args)
    return plain_body(*args)


def solution(mesh):
    return jax.shard_map(
        body,
        mesh=mesh,
        in_specs=(
            P("section", "replica", None, None),
            P("section", "replica", None, None),
            P("section", "replica", None),
            P("section", None, "replica"),
            P("section", "replica", None),
            P("section", None, "replica"),
            P("section"),
            P("replica", None),
        ),
        out_specs=(
            P("section", "replica", None),
            P("section", None, "replica"),
            P("section", "replica", None),
        ),
        check_vma=False,
    )
```

```python
import functools

import jax
import jax.numpy as jnp
from jax import lax
from jax.experimental import pallas as pl
from jax.experimental.pallas import tpu as pltpu
from jax.sharding import PartitionSpec as P


def shifted(block, axis, distance):
    devices = range(lax.axis_size(axis))
    route = [(i - distance, i) for i in devices if i - distance in devices]
    return lax.ppermute(block, axis, route)


def outer_update(master, moment, summed, replicas):
    mean_value = summed / replicas
    delta = master - mean_value
    moment_new = 0.9 * moment + delta
    return master - 0.7 * (delta + 0.9 * moment_new)


def plain_body(wa_local, wb_local, wa_master, wb_master, wa_moment, wb_moment, counts, inputs):
    replicas = lax.axis_size("replica")
    wa_summed, wb_summed = (
        lax.psum_scatter(
            wa_local[0, 0].astype(jnp.float32).astype(jnp.bfloat16),
            "replica",
            scatter_dimension=0,
            tiled=True,
        ).astype(jnp.float32),
        lax.psum_scatter(
            wb_local[0, 0].astype(jnp.float32).astype(jnp.bfloat16),
            "replica",
            scatter_dimension=1,
            tiled=True,
        ).astype(jnp.float32),
    )
    wa_next = outer_update(wa_master[0], wa_moment[0], wa_summed, replicas)
    wb_next = outer_update(wb_master[0], wb_moment[0], wb_summed, replicas)
    wa_full, wb_full = (
        lax.all_gather(wa_next.astype(jnp.bfloat16), "replica", axis=0, tiled=True),
        lax.all_gather(wb_next.astype(jnp.bfloat16), "replica", axis=1, tiled=True),
    )
    section_index = lax.axis_index("section")
    section_total = lax.axis_size("section")
    layer_count = counts[0]
    pieces = 2
    block_rows = inputs.shape[0] // pieces

    def apply_layer(step_index, stream):
        square_mean = jnp.mean(stream * stream, axis=-1, keepdims=True)
        normed = (stream * lax.rsqrt(square_mean + 1e-05)).astype(jnp.bfloat16)
        gate_value = jnp.dot(normed, wa_full, preferred_element_type=jnp.float32)
        hidden = jax.nn.silu(gate_value).astype(jnp.bfloat16)
        return stream + jnp.dot(hidden, wb_full, preferred_element_type=jnp.float32)

    def run_block(rows_in):
        stream = lax.fori_loop(0, layer_count, apply_layer, rows_in.astype(jnp.float32))
        return stream.astype(jnp.bfloat16)

    def skip_block(rows_in):
        return jnp.zeros_like(rows_in)

    def advance(step_index, incoming, output):
        offset_step = step_index - section_index
        active = jnp.logical_and(offset_step >= 0, offset_step < pieces)
        block_place = jnp.clip(offset_step, 0, pieces - 1) * block_rows
        fresh_rows = lax.dynamic_slice_in_dim(inputs, block_place, block_rows, 0)
        source = jnp.where(section_index == 0, fresh_rows, incoming)
        sent_block = lax.cond(active, run_block, skip_block, source)

        def write_block(current):
            return lax.dynamic_update_slice_in_dim(current, sent_block, block_place, 0)

        def keep_block(current):
            return current

        output = lax.cond(active, write_block, keep_block, output)
        return (sent_block, output)

    def step_body(step_index, state_pair):
        incoming, output = state_pair
        sent_block, output = advance(step_index, incoming, output)
        incoming = shifted(sent_block, "section", 1)
        return (incoming, output)

    step_count = section_total + pieces - 1
    start_rows = jnp.zeros((block_rows, inputs.shape[1]), jnp.bfloat16)
    start_output = jnp.zeros(inputs.shape, jnp.bfloat16)
    incoming, output = lax.fori_loop(0, step_count - 1, step_body, (start_rows, start_output))
    unused_block, output = advance(step_count - 1, incoming, output)
    return (wa_next[None], wb_next[None], output[None])


MESH = pl.DeviceIdType.MESH
MOST_LAYERS = 6


def fused_kernel(
    sections, pieces, cuts,
    la, lb, ma, va, mb, vb, inputs_t, counts,
    out_a, out_b, boundary_t,
    own_layers, inputs_here, layers, lodger, rp, sx, rx, lent, full_a, full_bt, wb_full, stream, rin, sent, held, state,
    held_sem, state_sem, small_sem,
    pair_send, pair_recv, own_pair_send, own_pair_recv,
    pass_send, pass_recv, relay_send, relay_recv,
    y_send, y_recv, lent_recv, back_send,
    mate_send, mate_recv, share_send, share_recv, aside_send, aside_recv,
):
    s = lax.axis_index("section")
    i = lax.axis_index("replica")
    core = lax.rem(i, 2)
    p = i + 1 - 2 * core
    q = lax.rem(i + 2, 4)
    pq = lax.rem(p + 2, 4)
    n = ma.shape[0]
    step = n // cuts
    tokens = rin.shape[0]
    rows = tokens // pieces
    wide = 128
    side = lax.rem(s, 2)
    mate = s + 1 - 2 * side
    first_paired = 2 * (sections // 4)
    paired = s >= first_paired
    last = s + 2 >= sections
    patient = jnp.logical_and(s >= 2, jnp.logical_not(last))
    yields = jnp.logical_and(paired, jnp.logical_not(last))
    lends = s >= 2
    borrows = s + 2 < sections
    interleaves = jnp.logical_or(paired, s == 1)

    def middle(section):
        return jnp.logical_and(section >= 2, section < first_paired)

    def over_z(section, share, phase):
        some = jnp.logical_and(section >= 0, section + 2 < sections)
        if share == 0 and phase == 1:
            return section < -sections
        if share == 0:
            return jnp.logical_and(some, middle(section))
        if phase == 1:
            return some
        return jnp.logical_and(some, jnp.logical_not(middle(section)))

    def over_x(section, share, k):
        return section == 0 if share == 0 and k == 0 else None

    local = (lb, la)
    result = (out_b, out_a)
    full = (full_bt.at[side], full_a.at[side])
    other_full = (full_bt.at[1 - side], full_a.at[1 - side])

    def slice_of(owner):
        return pl.ds(pl.multiple_of(owner * n, n), n)

    barrier = pltpu.get_barrier_semaphore()
    pl.semaphore_signal(barrier, inc=1, device_id=(s, p), device_id_type=MESH)
    pl.semaphore_signal(barrier, inc=1, device_id=(s, q), device_id_type=MESH)

    @pl.when(s > 0)
    def _():
        pl.semaphore_signal(barrier, inc=1, device_id=(s - 1, i), device_id_type=MESH)

    @pl.when(s < sections - 1)
    def _():
        pl.semaphore_signal(barrier, inc=1, device_id=(s + 1, i), device_id_type=MESH)

    @pl.when(lends)
    def _():
        pl.semaphore_signal(barrier, inc=1, device_id=(s - 2, i), device_id_type=MESH)
        pl.semaphore_signal(barrier, inc=1, device_id=(s - 2, q), device_id_type=MESH)

    @pl.when(borrows)
    def _():
        pl.semaphore_signal(barrier, inc=1, device_id=(s + 2, i), device_id_type=MESH)
        pl.semaphore_signal(barrier, inc=1, device_id=(s + 2, q), device_id_type=MESH)

    @pl.when(s < 2)
    def _():
        pl.semaphore_signal(barrier, inc=1, device_id=(1 - s, q), device_id_type=MESH)

    loads = {}
    for kind, owner in ((0, q), (1, i)):
        for t in range(2):
            load = pltpu.make_async_copy(local[t].at[slice_of(owner)], held.at[t, kind], held_sem.at[t, kind])
            load.start()
            loads[t, kind] = load

    layers_load = pltpu.make_async_copy(counts, own_layers, small_sem.at[0])
    layers_load.start()
    inputs_load = pltpu.make_async_copy(inputs_t, inputs_here, small_sem.at[1])

    @pl.when(s == 0)
    def _():
        inputs_load.start()

    greeted = jnp.maximum(2 - s, 0) - jnp.maximum(1 - s, 0) + jnp.minimum(s, 1) + jnp.minimum(sections - 1 - s, 1)
    greeted = greeted + 2 * jnp.minimum(s // 2, 1) + 2 * jnp.minimum((sections - 1 - s) // 2, 1)
    pl.semaphore_wait(barrier, 2 + greeted)

    def part(owner, k):
        return pl.ds(pl.multiple_of(owner * n + k * step, step), step)

    def remote(src, dst, send, recv, where):
        return pltpu.make_async_remote_copy(
            src_ref=src, dst_ref=dst, send_sem=send, recv_sem=recv,
            device_id=where, device_id_type=MESH,
        )

    order = [(t, k) for t in range(2) for k in range(cuts)]
    sends = []
    pair = {}
    for kind in range(2):
        for t, k in order:
            owner = pq if kind == 0 else p
            copy = remote(
                local[t].at[part(owner, k)],
                rp.at[t, kind, pl.ds(k * step, step)],
                pair_send.at[t, kind, k], pair_recv.at[t, kind, k], (s, p),
            )
            copy.start()
            pair[t, kind, k] = copy
            sends.append(copy)

    for t in range(2):
        for which, source in enumerate(((mb, vb), (ma, va))[t]):
            load = pltpu.make_async_copy(source, state.at[t, which], state_sem.at[t, which])
            load.start()
            loads[t, 2 + which] = load

    @pl.when(s == 0)
    def _():
        inputs_load.wait()
        for block in range(tokens // wide):
            there = pl.ds(block * wide, wide)
            rin[there, :] = inputs_here[:, there].T

    def portion(share, k):
        first = step // 3 * min(k + 1, 2)
        return (0, first) if share == 0 else (first, step - first)

    def share_rows(base, share, k):
        start, size = portion(share, k)
        return pl.ds(pl.multiple_of(base + k * step + start, 16), size)

    def ends(phase, share, t, k):
        if phase == 0:
            return sx.at[t, share_rows(0, share, k)], rx.at[t, share_rows(0, share, k)]
        there = full[t].at[share_rows(i * n, share, k)]
        return there, there

    def direct(phase, share, t, k):
        src, dst = ends(phase, share, t, k)
        return remote(src, dst, y_send.at[phase, share, t, k], y_recv.at[phase, share, t, k], (s, q))

    def lent_rows(phase, share, t, k):
        start, size = portion(share, k)
        return lent.at[phase, t, k, pl.ds(start, size)]

    def detour(phase, share, t, k, stride):
        src, dst = ends(phase, share, t, k)
        return remote(
            src, lent_rows(phase, share, t, k), y_send.at[phase, share, t, k], lent_recv.at[phase, share, t, k],
            (lax.rem(s + stride, sections), q),
        )

    def give_back(phase, share, t, k, stride):
        base = 0 if phase == 0 else q * n
        there = other_full[t] if stride == 1 else full[t]
        dst = (rx.at[t] if phase == 0 else there).at[share_rows(base, share, k)]
        return remote(
            lent_rows(phase, share, t, k), dst, back_send.at[phase, share, t, k], y_recv.at[phase, share, t, k],
            (lax.rem(s + sections - stride, sections), i),
        )

    def send_detours(phase, t, k):
        for share in range(2):
            @pl.when(over_z(s, share, phase))
            def _():
                detour(phase, share, t, k, 2).start()

            sideways = over_x(s, share, k)
            if sideways is not None:
                @pl.when(sideways)
                def _():
                    detour(phase, share, t, k, 1).start()

    def send_direct(phase, t, k, now):
        for share in range(2):
            stays_here = jnp.logical_not(over_z(s, share, phase))
            sideways = over_x(s, share, k)
            if sideways is not None:
                stays_here = jnp.logical_and(stays_here, jnp.logical_not(sideways))

            @pl.when(jnp.logical_and(now, stays_here))
            def _():
                direct(phase, share, t, k).start()

    def each_lent(phase, t, k, act):
        for share in range(2):
            @pl.when(over_z(s - 2, share, phase))
            def _():
                act(share, 2)

            sideways = over_x(s - 1, share, k)
            if sideways is not None:
                @pl.when(sideways)
                def _():
                    act(share, 1)

    def send_back(phase, now, which):
        for t, k in which:
            @pl.when(now)
            def _():
                def act(share, stride):
                    detour(phase, share, t, k, stride).wait_recv()
                    give_back(phase, share, t, k, stride).start()

                each_lent(phase, t, k, act)

    def to_mate(kind, t, k):
        there = part(q if kind else i, k)
        return remote(
            full[t].at[there], full[t].at[there], mate_send.at[kind, t, k], mate_recv.at[kind, t, k], (mate, i)
        )

    def to_partner(kind, t, k):
        there = part(q if kind else i, k)
        return remote(
            other_full[t].at[there], other_full[t].at[there],
            share_send.at[kind, t, k], share_recv.at[kind, t, k], (s, p),
        )

    def layers_aside():
        return remote(layers.at[side], layers.at[side], aside_send.at[0], aside_recv.at[0], (mate, i))

    def rows_aside(job):
        return remote(sent.at[job], lodger, aside_send.at[1], aside_recv.at[1], (mate, i))

    layers_load.wait()
    layers[side] = jnp.full(layers.shape[1:], own_layers[0]).astype(jnp.float32)

    @pl.when(paired)
    def _():
        layers_aside().start()

    for t, k in order:
        if k == 0:
            loads[t, 0].wait()
        pair[t, 0, k].wait_recv()
        here = pl.ds(k * step, step)
        total = held[t, 0, here, :].astype(jnp.float32) + rp[t, 0, here, :].astype(jnp.float32)
        sx[t, here, :] = total.astype(jnp.bfloat16)
        send_detours(0, t, k)
        send_direct(0, t, k, jnp.logical_not(patient))

    send_back(0, s >= 1, order)
    for t, k in order:
        send_direct(0, t, k, patient)
    send_back(1, jnp.logical_not(interleaves), order)

    lag = 3
    own_pair = {}
    for t, k in order:
        if k == 0:
            for which in (1, 2, 3):
                loads[t, which].wait()
        pair[t, 1, k].wait_recv()
        here = pl.ds(k * step, step)
        total = held[t, 1, here, :].astype(jnp.float32) + rp[t, 1, here, :].astype(jnp.float32)
        for share in range(2):
            direct(0, share, t, k).wait_recv()
        total = total + rx[t, here, :].astype(jnp.float32)
        fresh = outer_update(state[t, 0, here, :], state[t, 1, here, :], total, 4)
        result[t][here, :] = fresh
        mine = part(i, k)
        full[t][mine, :] = fresh.astype(jnp.bfloat16)
        send_detours(1, t, k)
        send_direct(1, t, k, True)
        copy = remote(
            full[t].at[mine], full[t].at[mine], own_pair_send.at[t, k], own_pair_recv.at[t, k], (s, p)
        )
        copy.start()
        own_pair[t, k] = copy
        sends.append(copy)

        @pl.when(paired)
        def _():
            to_mate(0, t, k).start()

        send_back(1, s == 1, [(t, k)])
        done = order.index((t, k)) + 1 - lag
        if done > 0:
            send_back(1, paired, [order[done - 1]])

    send_back(1, paired, order[len(order) - lag :])

    def collect(t):
        passed = []
        for k in range(cuts):
            for share in range(2):
                direct(1, share, t, k).wait_recv()
            other = part(q, k)
            copy = remote(
                full[t].at[other], full[t].at[other], pass_send.at[t, k], pass_recv.at[t, k], (s, p)
            )
            copy.start()
            passed.append(copy)
            sends.append(copy)

            @pl.when(paired)
            def _():
                to_mate(1, t, k).start()

        for k in range(cuts):
            own_pair[t, k].wait_recv()
            passed[k].wait_recv()

    def turn_over(slot):
        for k in range(wb_full.shape[1] // wide):
            there = pl.ds(k * wide, wide)
            wb_full[slot, there, :] = full_bt[slot, :, there].T

    collect(0)
    turn_over(side)
    collect(1)

    def take_in(kind, t):
        for k in range(cuts):
            to_mate(kind, t, k).wait_recv()
            to_partner(kind, t, k).start()

    def take_in_rest(t):
        take_in(1, t)
        for kind in range(2):
            for k in range(cuts):
                to_partner(kind, t, k).wait_recv()

    @pl.when(paired)
    def _():
        take_in(0, 0)
        take_in(0, 1)
        take_in_rest(0)
        turn_over(1 - side)
        layers_aside().wait_recv()

    late = jnp.logical_and(yields, side == 0)

    @pl.when(jnp.logical_and(paired, jnp.logical_not(late)))
    def _():
        take_in_rest(1)

    def piece_at(piece):
        return pl.ds(pl.multiple_of(piece * rows, rows), rows)

    def hop(job, piece, there):
        return remote(
            sent.at[job], rin.at[piece_at(piece)], relay_send.at[job], relay_recv.at[piece],
            (lax.rem(there, sections), i),
        )

    for job in range(2):
        piece = jnp.where(paired, side, job)
        slot = jnp.where(paired, job, side)
        stays = jnp.logical_and(paired, job == 1)

        if job == 1:
            @pl.when(late)
            def _():
                take_in_rest(1)

        @pl.when(jnp.logical_and(s > 0, jnp.logical_not(stays)))
        def _():
            hop(job, piece, s).wait_recv()

        @pl.when(stays)
        def _():
            stream[...] = sent[0].astype(jnp.float32)

        @pl.when(jnp.logical_not(stays))
        def _():
            stream[...] = rin[piece_at(piece), :].astype(jnp.float32)

        def apply_layer(layer, carry):
            x = stream[...]
            scale = lax.rsqrt(jnp.mean(x * x, axis=-1, keepdims=True) + 1e-05)
            gate = jnp.dot(x.astype(jnp.bfloat16), full_a[slot], preferred_element_type=jnp.float32)
            half = gate * (0.5 * scale)
            hidden = (half + half * jnp.tanh(half)).astype(jnp.bfloat16)
            change = jnp.dot(hidden, wb_full[slot], preferred_element_type=jnp.float32)
            active = jnp.broadcast_to(layers[slot, 0:1, 0:1], change.shape) > layer
            stream[...] = x + jnp.where(active, change, 0.0)
            return carry

        lax.fori_loop(0, MOST_LAYERS, apply_layer, 0, unroll=MOST_LAYERS)
        sent[job] = stream[...].astype(jnp.bfloat16)

        if job == 1:
            @pl.when(jnp.logical_and(paired, s + 2 < sections))
            def _():
                hop(job, piece, s + 2).start()

        @pl.when(jnp.logical_not(paired))
        def _():
            hop(job, piece, s + 1 + job * (s + 1 == first_paired)).start()

        @pl.when(jnp.logical_and(paired, side != job))
        def _():
            rows_aside(job).start()

    @pl.when(jnp.logical_not(paired))
    def _():
        boundary_t[:, piece_at(0)] = sent[0].T
        boundary_t[:, piece_at(1)] = sent[1].T

    @pl.when(paired)
    def _():
        boundary_t[:, piece_at(side)] = sent[side].T
        rows_aside(0).wait_recv()
        boundary_t[:, piece_at(1 - side)] = lodger[...].T

    for copy in sends:
        copy.wait_send()
    for phase in range(2):
        for t, k in order:
            for share in range(2):
                direct(phase, share, t, k).wait_send()

            def act(share, stride):
                give_back(phase, share, t, k, stride).wait_send()

            each_lent(phase, t, k, act)

    @pl.when(jnp.logical_not(paired))
    def _():
        hop(0, 0, s).wait_send()

    @pl.when(jnp.logical_or(jnp.logical_not(paired), s + 2 < sections))
    def _():
        hop(1, 0, s).wait_send()

    @pl.when(paired)
    def _():
        rows_aside(0).wait_send()
        layers_aside().wait_send()
        for kind in range(2):
            for t, k in order:
                to_mate(kind, t, k).wait_send()
                to_partner(kind, t, k).wait_send()


def hand_out_kernel(parts, *refs):
    count = len(refs) // 3
    writes = []
    for source, result, sem in zip(refs[:count], refs[count : 2 * count], refs[2 * count :]):
        step = result.shape[0] // parts
        for k in range(parts):
            here = pl.ds(k * step, step)
            write = pltpu.make_async_copy(source.at[here], result.at[here], sem.at[k])
            write.start()
            writes.append(write)
    for write in writes:
        write.wait()


def hand_out(*arrays):
    parts = 6
    return pl.pallas_call(
        functools.partial(hand_out_kernel, parts),
        out_shape=tuple(jax.ShapeDtypeStruct(a.shape, a.dtype) for a in arrays),
        in_specs=[pl.BlockSpec(memory_space=pl.ANY)] * len(arrays),
        out_specs=(pl.BlockSpec(memory_space=pl.ANY),) * len(arrays),
        scratch_shapes=[pltpu.SemaphoreType.DMA((parts,))] * len(arrays),
    )(*(pltpu.with_memory_space_constraint(a, pltpu.VMEM) for a in arrays))


def fused_body(wa_local, wb_local, wa_master, wb_master, wa_moment, wb_moment, counts, inputs):
    sections = lax.axis_size("section")
    n, wide = wa_master.shape[1:]
    depth = wa_local.shape[2]
    tokens = inputs.shape[0]
    pieces = 2
    cuts = 3
    f32, bf16 = jnp.float32, jnp.bfloat16
    vmem = pl.BlockSpec(memory_space=pltpu.VMEM)
    anywhere = pl.BlockSpec(memory_space=pl.ANY)
    sems = pltpu.SemaphoreType.DMA
    wa_next, wb_next_t, boundary_t = pl.pallas_call(
        functools.partial(fused_kernel, sections, pieces, cuts),
        out_shape=(
            pltpu.VMEM((n, wide), f32),
            pltpu.VMEM((n, wide), f32),
            pltpu.VMEM((depth, tokens), bf16),
        ),
        in_specs=[anywhere] * 8,
        out_specs=(vmem, vmem, vmem),
        scratch_shapes=[
            pltpu.SMEM((1,), jnp.int32),
            pltpu.VMEM((depth, tokens), bf16),
            pltpu.VMEM((2, 8, 128), f32),
            pltpu.VMEM((tokens // pieces, depth), bf16),
            pltpu.VMEM((2, 2, n, wide), bf16),
            pltpu.VMEM((2, n, wide), bf16),
            pltpu.VMEM((2, n, wide), bf16),
            pltpu.VMEM((2, 2, cuts, n // cuts, wide), bf16),
            pltpu.VMEM((2, depth, wide), bf16),
            pltpu.VMEM((2, depth, wide), bf16),
            pltpu.VMEM((2, wide, depth), bf16),
            pltpu.VMEM((tokens // pieces, depth), f32),
            pltpu.VMEM((tokens, depth), bf16),
            pltpu.VMEM((pieces, tokens // pieces, depth), bf16),
            pltpu.VMEM((2, 2, n, wide), bf16),
            pltpu.VMEM((2, 2, n, wide), f32),
            sems((2, 2)), sems((2, 2)), sems((2,)),
            sems((2, 2, cuts)), sems((2, 2, cuts)),
            sems((2, cuts)), sems((2, cuts)),
            sems((2, cuts)), sems((2, cuts)),
            sems((pieces,)), sems((pieces,)),
            sems((2, 2, 2, cuts)), sems((2, 2, 2, cuts)),
            sems((2, 2, 2, cuts)), sems((2, 2, 2, cuts)),
            sems((2, 2, cuts)), sems((2, 2, cuts)),
            sems((2, 2, cuts)), sems((2, 2, cuts)),
            sems((2,)), sems((2,)),
        ],
        compiler_params=pltpu.CompilerParams(
            collective_id=0, has_side_effects=True, vmem_limit_bytes=56 * 1024 * 1024,
        ),
    )(
        wa_local[0, 0], wb_local[0, 0].T,
        wa_master[0], wa_moment[0], wb_master[0].T, wb_moment[0].T,
        inputs.T, counts,
    )
    wa_next, wb_next_t, boundary_t = hand_out(wa_next, wb_next_t, boundary_t)
    return (wa_next[None], wb_next_t.T[None], boundary_t.T[None])


def body(*args):
    rows = args[2].shape[1]
    sections = lax.axis_size("section")
    tokens = args[7].shape[0]
    if lax.axis_size("replica") == 4 and sections % 2 == 0 and sections >= 4 and rows % 144 == 0 and tokens % 256 == 0:
        return fused_body(*args)
    return plain_body(*args)


def solution(mesh):
    return jax.shard_map(
        body,
        mesh=mesh,
        in_specs=(
            P("section", "replica", None, None),
            P("section", "replica", None, None),
            P("section", "replica", None),
            P("section", None, "replica"),
            P("section", "replica", None),
            P("section", None, "replica"),
            P("section"),
            P("replica", None),
        ),
        out_specs=(
            P("section", "replica", None),
            P("section", None, "replica"),
            P("section", "replica", None),
        ),
        check_vma=False,
    )
```
